128 devices in a mesh: gx: 8 (over x, core), yz: 16 (over y, z).
Axes of the slice: x: 4, y: 4, z: 4, core: 2. Of those that a mesh axis runs over, the one named last changes fastest.
Arguments:
- right_side: float32 [3, 64, 2048, 256], P(None, 'gx', 'yz'), may hold values from -30 to 30
- viscosity: bfloat16 [64, 2048, 256], P('gx', 'yz'), may hold values from 0.29882812 to 3
- strain_rate: bfloat16 [6, 64, 2048, 256], P(None, 'gx', 'yz'), may hold values from -6 to 6
- cell_code: int32 [64, 2048, 256], P('gx', 'yz'), may hold values from 0 to 2
Outputs:
- solution_field: float32 [3, 64, 2048, 256], P(None, 'gx', 'yz')
- residual: float32 [3, 64, 2048, 256], P(None, 'gx', 'yz')
The draws below stay inside these ranges and needn't reach their ends.
All inputs are finite; a program needn't handle non-finite values.
Results may differ from the reference program's by a relative error of at most 0.0003.
Values may be sent and summed in bfloat16 or wider, within the bound.
No kernel may reach another device: no remote copies, remote signals or barrier semaphores. Data moves between devices by JAX's collectives and lax.ppermute only.
A program may use at most 128 MiB of HBM per device.

```python
import math
import jax
import jax.numpy as jnp

ITERS = 3
NX = 64
NY = 2048
NZ = 256


def draw_right_side(key, part):
    keys = jax.random.split(key, 3)
    xpos = jnp.arange(NX, dtype=jnp.float32) / NX
    ypos = jnp.arange(NY, dtype=jnp.float32) / NY
    ramp = jnp.exp(jnp.log(3.0) * 0.5 * (xpos[:, None, None] + ypos[None, :, None]))
    value = jax.random.normal(keys[2], (3, NX, NY, NZ), jnp.float32) * ramp[None]
    return jnp.clip(value, -30.0, 30.0)


def place_ends(array, key, smallest, largest):
    longest = array.shape.index(max(array.shape))
    spots = []
    for shift in (0, 1):
        where = [jax.random.randint(jax.random.fold_in(key, axis), (), 0, length) for axis, length in enumerate(array.shape)]
        where[longest] = (where[longest] + shift) % array.shape[longest]
        spots.append(tuple(where))
    return array.at[spots[0]].set(smallest).at[spots[1]].set(largest)


def steps_of(stream_key, shape, cuts, smallest, high):
    gain, own = 1.0, jax.random.fold_in(stream_key, 6)
    for dim, shards_of in cuts:
        heights = jnp.exp(jax.random.uniform(jax.random.fold_in(own, dim), (shards_of,), jnp.float32, smallest / len(cuts), high / len(cuts)))
        gain = gain * jnp.repeat(heights, shape[dim] // shards_of).reshape([-1 if axis == dim else 1 for axis in range(len(shape))])
    return gain


def gaussian(own_key, dims, deviation, reach, pieces=(), kind=jnp.bfloat16):
    level = steps_of(own_key, dims, pieces, -0.22, 0.18) if pieces else 1.0
    values = jax.random.normal(own_key, dims, jnp.float32) * deviation * level
    return jnp.minimum(jnp.maximum(values, -reach), reach).astype(kind)


def setup_inputs(seed: int = 0) -> dict:
    splits = jax.random.split(jax.random.key(seed), 5)
    return {
        "right_side": draw_right_side(jax.random.fold_in(splits[4], 71), 0),
        "viscosity": jnp.clip(jnp.exp(math.log(3.0) - 2.306499 * jax.random.uniform(splits[1], (NX, NY, NZ), jnp.float32) ** steps_of(splits[1], (NX, NY, NZ), ((0, 8), (1, 16)), -0.2, 0.2)), 0.29882812, 3.0).astype(jnp.bfloat16),
        "strain_rate": gaussian(splits[2], (6, NX, NY, NZ), 1.0, 6.0, ((1, 8), (2, 16))),
        "cell_code": place_ends(jax.random.randint(splits[3], (NX, NY, NZ), 0, 3), jax.random.fold_in(splits[3], 1), 0, 2).astype(jnp.int32),
    }


SOFTEN = 0.8


def stresses(base, next_x, next_y, next_z, viscosity, strain_rate):
    along_x = next_x - base
    along_y = next_y - base
    along_z = next_z - base
    strain = strain_rate.astype(jnp.float32)
    two_eta = 2.0 * viscosity.astype(jnp.float32)
    parts = [along_x[0], along_y[1], along_z[2], 0.5 * (along_y[0] + along_x[1]), 0.5 * (along_z[0] + along_x[2]), 0.5 * (along_z[1] + along_y[2])]
    self_dot = strain[0] * strain[0] + strain[1] * strain[1] + strain[2] * strain[2] + 2.0 * (strain[3] * strain[3] + strain[4] * strain[4] + strain[5] * strain[5])
    cross_dot = strain[0] * parts[0] + strain[1] * parts[1] + strain[2] * parts[2] + 2.0 * (strain[3] * parts[3] + strain[4] * parts[4] + strain[5] * parts[5])
    factor = SOFTEN * cross_dot / (1.0 + self_dot)
    taus = [two_eta * (parts[k] - factor * strain[k]) for k in range(6)]
    flux_x = jnp.stack([taus[0], taus[3], taus[4]])
    flux_y = jnp.stack([taus[3], taus[1], taus[5]])
    flux_z = jnp.stack([taus[4], taus[5], taus[2]])
    return flux_x, flux_y, flux_z


def divergence(own_x, prev_x, own_y, prev_y, own_z, prev_z):
    return (prev_x - own_x) + (prev_y - own_y) + (prev_z - own_z)


def coefficients(cell_code):
    mask = (cell_code != 0).astype(jnp.float32)
    weight = jnp.where(cell_code == 0, 1.0, jnp.where(cell_code == 1, 0.2, 1.2)).astype(jnp.float32)
    return mask, weight


def operate(field, viscosity, strain_rate, mask, weight):
    masked = mask * field
    zero_x = jnp.zeros_like(masked[:, :1])
    zero_y = jnp.zeros_like(masked[:, :, :1])
    zero_z = jnp.zeros_like(masked[..., :1])
    next_x = jnp.concatenate([masked[:, 1:], zero_x], 1)
    next_y = jnp.concatenate([masked[:, :, 1:], zero_y], 2)
    next_z = jnp.concatenate([masked[..., 1:], zero_z], 3)
    flux_x, flux_y, flux_z = stresses(masked, next_x, next_y, next_z, viscosity, strain_rate)
    prev_x = jnp.concatenate([zero_x, flux_x[:, :-1]], 1)
    prev_y = jnp.concatenate([zero_y, flux_y[:, :, :-1]], 2)
    prev_z = jnp.concatenate([zero_z, flux_z[..., :-1]], 3)
    return mask * divergence(flux_x, prev_x, flux_y, prev_y, flux_z, prev_z) + weight * field


def reference(right_side, viscosity, strain_rate, cell_code):
    mask, weight = coefficients(cell_code)
    solution_field = jnp.zeros_like(right_side)
    residual = right_side
    direction = right_side
    norm_now = jnp.sum(residual * residual)
    for iteration in range(ITERS):
        image = operate(direction, viscosity, strain_rate, mask, weight)
        alpha = norm_now / jnp.sum(direction * image)
        solution_field = solution_field + alpha * direction
        residual = residual - alpha * image
        norm_next = jnp.sum(residual * residual)
        direction = residual + (norm_next / norm_now) * direction
        norm_now = norm_next
    return solution_field, residual
```

```python
import jax
import jax.numpy as jnp
from jax import lax
from jax.experimental import pallas as pl
from jax.experimental.pallas import tpu as pltpu
from jax.sharding import PartitionSpec as P

SOFTEN = 0.8
F32 = jnp.float32
BF16 = jnp.bfloat16
LANES = 128
ROWS = 8
VMEM = pltpu.VMEM


def resident(shape, dtype=F32):
    return VMEM(shape, dtype)


def in_vmem(x):
    return pltpu.with_memory_space_constraint(x, VMEM)


def call(kernel, name, ins, outs, scratch=(), aliases=None, limit=24, cost=(1e6, 1e6)):
    specs, args = [], []
    for kind, x in ins:
        if kind == "hbm":
            specs.append(pl.BlockSpec(memory_space=pl.ANY))
            args.append(x)
        elif kind == "smem":
            specs.append(pl.BlockSpec(memory_space=pltpu.SMEM))
            args.append(x)
        else:
            specs.append(pl.BlockSpec(memory_space=VMEM))
            args.append(in_vmem(x))
    out_specs = [
        pl.BlockSpec(memory_space=VMEM) if isinstance(o, type(VMEM((8, 128), F32))) else pl.BlockSpec(memory_space=pl.ANY)
        for o in outs
    ]
    return pl.pallas_call(
        kernel,
        name=name,
        out_shape=outs,
        in_specs=specs,
        out_specs=out_specs,
        scratch_shapes=list(scratch),
        input_output_aliases=aliases or {},
        compiler_params=pltpu.CompilerParams(vmem_limit_bytes=limit << 20),
        cost_estimate=pl.CostEstimate(flops=int(cost[0]), bytes_accessed=int(cost[1]), transcendentals=0),
    )(*args)


def iotas():
    row = lax.broadcasted_iota(jnp.int32, (ROWS, LANES), 0)
    lane = lax.broadcasted_iota(jnp.int32, (ROWS, LANES), 1)
    return row, lane


def at(t, h):
    return pl.ds(ROWS * t, ROWS), pl.ds(LANES * h, LANES)


def weight_of(code):
    return jnp.where(code == 0, 0.0, jnp.where(code == 1, 0.2, 1.2)).astype(F32)


def tensor_of(visc, strain):
    two_eta = 2.0 * visc
    square = (
        strain[0] * strain[0]
        + strain[1] * strain[1]
        + strain[2] * strain[2]
        + 2.0 * (strain[3] * strain[3] + strain[4] * strain[4] + strain[5] * strain[5])
    )
    scale = jnp.sqrt(SOFTEN * two_eta / (1.0 + square))
    return [two_eta] + [scale * s for s in strain]


def split(x):
    high = x.astype(BF16)
    return high, (x - high.astype(F32)).astype(BF16)


def pack_kernel(par, b, visc, strain, code, ya, yb, xa, xb, tb, tv, ts, tc, lb, lc, sem):
    nl, nrow = b.shape[1], b.shape[2]
    copies = []
    for i, r in enumerate((0, nrow - ROWS)):
        rows = pl.ds(r, ROWS)
        copies.append(pltpu.make_async_copy(b.at[:, :, rows, :], tb.at[i], sem.at[i, 0]))
        copies.append(pltpu.make_async_copy(visc.at[:, rows, :], tv.at[i], sem.at[i, 1]))
        copies.append(pltpu.make_async_copy(strain.at[:, :, rows, :], ts.at[i], sem.at[i, 2]))
        copies.append(pltpu.make_async_copy(code.at[:, rows, :], tc.at[i], sem.at[i, 3]))
    px = par[0]
    py = par[1]
    late = []
    for i, out in enumerate((xa, xb)):
        layer = jnp.where(px == i, nl - 1, 0)
        copies.append(pltpu.make_async_copy(b.at[:, layer], lb.at[i], sem.at[i, 4]))
        copies.append(pltpu.make_async_copy(code.at[layer], lc.at[i], sem.at[i, 5]))
        late.append(pltpu.make_async_copy(visc.at[layer], out.at[6], sem.at[i, 6]))
        late.append(pltpu.make_async_copy(strain.at[:, layer], out.at[pl.ds(7, 6)], sem.at[i, 7]))
    for c in copies + late:
        c.start()
    for c in copies:
        c.wait()
    for i, out in enumerate((ya, yb)):
        slot = jnp.where(py == i, 1, 0)
        for l in range(nl):
            held = tc[slot, l] == 0
            for k in range(3):
                high, low = split(jnp.where(held, 0.0, tb[slot, k, l]))
                out[k, l] = high
                out[3 + k, l] = low
            out[6, l] = tv[slot, l]
            for k in range(6):
                out[7 + k, l] = ts[slot, k, l]
            out[13, l] = tc[slot, l].astype(F32).astype(BF16)
    for i, out in enumerate((xa, xb)):
        for t in range(nrow // 16):
            rows = pl.ds(16 * t, 16)
            held = lc[i, rows, :] == 0
            for k in range(3):
                high, low = split(jnp.where(held, 0.0, lb[i, k, rows, :]))
                out[k, rows, :] = high
                out[3 + k, rows, :] = low
    for c in late:
        c.wait()


def load_kernel(b, visc, strain, code, raw, es, m0, w, acc, sv, ss, sc, sem):
    nl, nrow = b.shape[1], b.shape[2]
    copies = []
    for l in range(nl):
        copies.append(
            [
                pltpu.make_async_copy(b.at[:, l], raw.at[:, l], sem.at[l, 0]),
                pltpu.make_async_copy(visc.at[l], sv.at[l], sem.at[l, 1]),
                pltpu.make_async_copy(strain.at[:, l], ss.at[l], sem.at[l, 2]),
                pltpu.make_async_copy(code.at[l], sc.at[l], sem.at[l, 3]),
            ]
        )
        for c in copies[-1]:
            c.start()
    zero = jnp.zeros((ROWS, LANES), F32)

    def chunk(l, u, carry):
        sums, helds = carry
        base = pl.multiple_of(16 * u, 16)
        rows16 = pl.ds(base, 16)
        v16 = sv[l, rows16, :].astype(F32)
        s16 = [ss[l, k, rows16, :].astype(F32) for k in range(6)]
        for i in range(2):
            for h in range(2):
                cut = lambda x: x[ROWS * i : ROWS * (i + 1), LANES * h : LANES * (h + 1)]
                rows, cols = pl.ds(pl.multiple_of(base + ROWS * i, ROWS), ROWS), pl.ds(LANES * h, LANES)
                weight = weight_of(sc[l, rows, cols])
                w[l, rows, cols] = weight
                for k, value in enumerate(tensor_of(cut(v16), [cut(s) for s in s16])):
                    es[l, k, rows, cols] = value
                for k in range(3):
                    x = raw[k, l, rows, cols]
                    m = jnp.where(weight > 0.0, x, 0.0)
                    m0[k, l, rows, cols] = m
                    rest = x - m
                    sums = sums + m * m
                    helds = helds + rest * rest
        return sums, helds

    carry = (zero, zero)
    for l in range(nl):
        for c in copies[l]:
            c.wait()
        carry = lax.fori_loop(0, nrow // 16, lambda u, s: chunk(l, u, s), carry)
    acc[0] = carry[0]
    acc[1] = carry[1]


def halo_kernel(par, ra, rb, es_in, m0_in, w_in, es, m0, w, ca, cb):
    row, _ = iotas()
    row2 = lax.broadcasted_iota(jnp.int32, (ROWS, 2 * LANES), 0)
    nl = ra.shape[1]
    halo = es.shape[2] - ROWS
    px = par[0]
    py = par[1]
    rows = pl.ds(halo, ROWS)

    def pick(k, l):
        a, c = ra[k, l].astype(F32), rb[k, l].astype(F32)
        even = (py == 0).astype(jnp.int32) + jnp.zeros_like(row2)
        upper = jnp.where(even == 1, a, c)
        lower = jnp.where(even == 1, c, a)
        return jnp.where(row2 < 3, upper, jnp.where(row2 >= 5, lower, 0.0))

    def layer(l, _):
        got = [pick(k, l) for k in range(14)]
        w[l, rows, :] = weight_of(got[13])
        for k, value in enumerate(tensor_of(got[6], got[7:13])):
            es[l, k, rows, :] = value
        for k in range(3):
            m0[k, l, rows, :] = got[k] + got[3 + k]
        return 0

    lax.fori_loop(0, nl, layer, 0)
    for i, out in enumerate((ca, cb)):
        l = jnp.where(px == i, nl - 1, 0)
        for k in range(13):
            out[k] = pick(k, l).astype(BF16)


def strain_parts(c, n, ynext, znext):
    ax = [n[k] - c[k] for k in range(3)]
    ay = [ynext[k] - c[k] for k in range(3)]
    az = [znext[k] - c[k] for k in range(3)]
    return [ax[0], ay[1], az[2], ay[0] + ax[1], az[0] + ax[2], az[1] + ay[2]]


def stress(parts, tensor, which):
    two_eta, s = tensor[0], tensor[1:]
    cross = (
        (s[0] * parts[0] + s[1] * parts[1])
        + (s[2] * parts[2] + s[3] * parts[3])
        + (s[4] * parts[4] + s[5] * parts[5])
    )
    eta = 0.5 * two_eta
    return {k: (two_eta if k < 3 else eta) * parts[k] - cross * s[k] for k in which}


class Plane:
    def __init__(self, center, following, tensor, tiles):
        self.center, self.following, self.tensor, self.tiles = center, following, tensor, tiles
        self.row, self.lane = iotas()
        self.cache = {}

    def tile(self, t):
        if t not in self.cache:
            m = [[self.center(k, t, h) for k in range(3)] for h in range(2)]
            r = [[pltpu.roll(m[h][k], ROWS - 1, 0) for k in range(3)] for h in range(2)]
            self.cache = {k: v for k, v in self.cache.items() if k == (t - 1) % self.tiles}
            self.cache[t] = (m, r)
        return self.cache[t]

    def stresses(self, t, which):
        m, r = self.tile(t)
        _, rn = self.tile((t + 1) % self.tiles)
        z = [[pltpu.roll(m[h][k], LANES - 1, 1) for k in range(3)] for h in range(2)]
        out = []
        for h in range(2):
            ynext = [jnp.where(self.row == ROWS - 1, rn[h][k], r[h][k]) for k in range(3)]
            znext = [jnp.where(self.lane == LANES - 1, z[1][k] if h == 0 else 0.0, z[h][k]) for k in range(3)]
            n = [self.following(k, t, h) for k in range(3)]
            parts = strain_parts(m[h], n, ynext, znext)
            out.append(stress(parts, [self.tensor(k, t, h) for k in range(7)], which))
        return m, out


FLUX_X, FLUX_Y, FLUX_Z = (0, 3, 4), (3, 1, 5), (4, 5, 2)


def full_plane(plane, tx, weight, write, own):
    row, lane, tiles = plane.row, plane.lane, plane.tiles
    halo = tiles - 1
    before = None
    kept = None

    def flux(t):
        m, tau = plane.stresses(t, range(6))
        y = [[tau[h][j] for j in FLUX_Y] for h in range(2)]
        ry = [[pltpu.roll(v, 1, 0) for v in y[h]] for h in range(2)]
        rz = [[pltpu.roll(tau[h][j], 1, 1) for j in FLUX_Z] for h in range(2)]
        div = []
        for h in range(2):
            rows, cols = at(t, h)
            line = []
            for k in range(3):
                x = tau[h][FLUX_X[k]]
                prev_z = jnp.where(lane == 0, rz[0][k] if h == 1 else 0.0, rz[h][k])
                line.append((tx[k, rows, cols] - x) + (prev_z - tau[h][FLUX_Z[k]]) - y[h][k])
                tx[k, rows, cols] = x
            div.append(line)
        return m, ry, div

    def finish(t, m, ry, div, prev):
        for h in range(2):
            rows, cols = at(t, h)
            wt = weight(t, h)
            new = [
                jnp.where(
                    wt > 0.0,
                    div[h][k] + jnp.where(row == 0, prev[h][k], ry[h][k]) + wt * m[h][k],
                    0.0,
                )
                for k in range(3)
            ]
            for k in range(3):
                write(k, t, h, new[k])
            if t != halo and own is not None:
                own(t, h, m[h], new)

    kept = flux(halo)
    before = kept[1]
    for t in range(halo):
        m, ry, div = flux(t)
        finish(t, m, ry, div, before)
        before = ry
    finish(halo, kept[0], kept[1], kept[2], before)


def lower_flux(plane, emit):
    for t in range(plane.tiles):
        _, tau = plane.stresses(t, FLUX_X)
        for h in range(2):
            emit(t, h, [tau[h][j] for j in FLUX_X])


class Sums:
    def __init__(self, init):
        self.cross = list(init[0])
        self.square = list(init[1])

    def add(self, t, h, old, new):
        i = (2 * t + h) % len(self.cross)
        for k in range(3):
            self.cross[i] = self.cross[i] + old[k] * new[k]
            self.square[i] = self.square[i] + new[k] * new[k]

    def state(self):
        return (tuple(self.cross), tuple(self.square))


def interior_kernel(m, es, w, v, tx_out, acc):
    nl, tiles = m.shape[1], m.shape[2] // ROWS
    zero = jnp.zeros((ROWS, LANES), F32)
    tx_out[...] = jnp.zeros(tx_out.shape, F32)

    def layer(l, carry):
        sums = Sums(carry)
        plane = Plane(
            lambda k, t, h: m[(k, l) + at(t, h)],
            lambda k, t, h: m[(k, l + 1) + at(t, h)],
            lambda k, t, h: es[(l, k) + at(t, h)],
            tiles,
        )

        def write(k, t, h, value):
            v[(k, l) + at(t, h)] = value

        full_plane(plane, tx_out, lambda t, h: w[(l,) + at(t, h)], write, sums.add)
        keep = jnp.where(l > 0, 1.0, 0.0).astype(F32)
        return jax.tree.map(lambda s: s * keep, sums.state())

    start = ((zero, zero), (zero, zero))
    cross, square = lax.fori_loop(0, nl - 1, layer, start)
    acc[0] = cross[0] + cross[1]
    acc[1] = square[0] + square[1]


def boundary_body(px, m, es, w, lo, hi, low_tensor, v_in, tx_in, acc_in, v, tx, acc):
    nl, tiles = m.shape[1], m.shape[2] // ROWS
    last = nl - 1
    zero = jnp.zeros((ROWS, LANES), F32)
    sums = Sums(((zero, zero), (zero, zero)))

    below = Plane(lo, lambda k, t, h: m[(k, 0) + at(t, h)], low_tensor, tiles)

    def emit(t, h, flux):
        wt = w[(0,) + at(t, h)]
        new = []
        for k in range(3):
            value = v_in[(k, 0) + at(t, h)] + jnp.where(wt > 0.0, flux[k], 0.0)
            v[(k, 0) + at(t, h)] = value
            new.append(value)
        if t != tiles - 1:
            sums.add(t, h, [m[(k, 0) + at(t, h)] for k in range(3)], new)

    lower_flux(below, emit)
    for k in range(3):
        tx[k] = tx_in[k]
    top = Plane(
        lambda k, t, h: m[(k, last) + at(t, h)],
        hi,
        lambda k, t, h: es[(last, k) + at(t, h)],
        tiles,
    )

    def write(k, t, h, value):
        v[(k, last) + at(t, h)] = value

    full_plane(top, tx, lambda t, h: w[(last,) + at(t, h)], write, sums.add)
    acc[0] = acc_in[0] + sums.cross[0] + sums.cross[1]
    acc[1] = acc_in[1] + sums.square[0] + sums.square[1]


def choose(flag, a, b):
    return jnp.where(flag + jnp.zeros(a.shape, jnp.int32) == 1, a, b)


def send_planes(px, v, ea, eb):
    last = v.shape[1] - 1
    for i, out in enumerate((ea, eb)):
        l = jnp.where(px == i, last, 0)
        for k in range(3):
            out[k] = v[k, l]


def first_boundary_kernel(par, m, es, w, xa, xb, ca, cb, v_in, tx_in, acc_in, v, acc, low, ea, eb, lo_s, hi_s, tx):
    px = par[0]
    even = (px == 0).astype(jnp.int32)
    nrow = xa.shape[1]

    def unpack(a, b, rows, n):
        def side(k, up):
            x, y = a(k), b(k)
            return choose(even, x, y) if up else choose(even, y, x)

        for k in range(3):
            hi_s[k, rows, :] = side(k, True) + side(3 + k, True)
            lo_s[k, rows, :] = side(k, False) + side(3 + k, False)
        tensor = tensor_of(side(6, False), [side(7 + k, False) for k in range(6)])
        for k in range(7):
            low[k, rows, :] = tensor[k]

    for t in range(nrow // 16):
        rows = pl.ds(16 * t, 16)
        unpack(lambda k: xa[k, rows, :].astype(F32), lambda k: xb[k, rows, :].astype(F32), rows, 16)
    unpack(lambda k: ca[k].astype(F32), lambda k: cb[k].astype(F32), pl.ds(nrow, ROWS), ROWS)
    boundary_body(
        px, m, es, w,
        lambda k, t, h: lo_s[(k,) + at(t, h)],
        lambda k, t, h: hi_s[(k,) + at(t, h)],
        lambda k, t, h: low[(k,) + at(t, h)],
        v_in, tx_in, acc_in, v, tx, acc,
    )
    send_planes(px, v, ea, eb)


def later_boundary(par, m, es, w, low, ra, rb, v_in, tx_in, acc_in, v, acc, tx):
    px = par[0]
    even = (px == 0).astype(jnp.int32)
    lo = lambda k, t, h: choose(even, rb[(k,) + at(t, h)], ra[(k,) + at(t, h)])
    hi = lambda k, t, h: choose(even, ra[(k,) + at(t, h)], rb[(k,) + at(t, h)])
    boundary_body(px, m, es, w, lo, hi, lambda k, t, h: low[(k,) + at(t, h)], v_in, tx_in, acc_in, v, tx, acc)


def second_boundary_kernel(par, m, es, w, low, ra, rb, v_in, tx_in, acc_in, v, acc, ea, eb, tx):
    later_boundary(par, m, es, w, low, ra, rb, v_in, tx_in, acc_in, v, acc, tx)
    send_planes(par[0], v, ea, eb)


def third_boundary_kernel(
    par, m, es, w, low, ra, rb, v_in, tx_in, acc_in, acc0, acc1, acc2, v, parts, tx, acc
):
    later_boundary(par, m, es, w, low, ra, rb, v_in, tx_in, acc_in, v, acc, tx)
    _, lane = iotas()
    line = jnp.zeros((ROWS, LANES), F32)
    terms = [acc0[0], acc0[1], acc1[0], acc1[1], acc2[0], acc2[1], acc[0]]
    for i, value in enumerate(terms):
        total = jnp.sum(jnp.sum(value, axis=0, keepdims=True), axis=1, keepdims=True)
        line = jnp.where(lane == i, total, line)
    for t in range(parts.shape[0] // ROWS):
        parts[pl.ds(ROWS * t, ROWS), :] = line


def coefficients(moment):
    size = 4
    zero = None

    def dot(a, b, shift):
        total = None
        for i in range(size):
            for j in range(size):
                if a[i] is None or b[j] is None:
                    continue
                term = a[i] * b[j] * moment[i + j + shift]
                total = term if total is None else total + term
        return total

    def axpy(a, scale, b):
        out = []
        for x, y in zip(a, b):
            term = None if y is None else scale * y
            out.append(x if term is None else term if x is None else x + term)
        return out

    one = jnp.ones_like(moment[0])
    residual = [one, zero, zero, zero]
    direction = list(residual)
    field = [zero] * size
    now = moment[0]
    for iteration in range(3):
        alpha = now / dot(direction, direction, 1)
        field = axpy(field, alpha, direction)
        if iteration == 2:
            break
        residual = axpy(residual, -alpha, [None] + direction[: size - 1])
        following = dot(residual, residual, 0)
        direction = axpy(residual, following / now, direction)
        now = following
    return field[:3]


def output_kernel(gathered, raw, w, m1, m2, m3, x, r, xs, rs, sem):
    nl, nrow = raw.shape[1], raw.shape[2]
    total = jnp.sum(gathered[...], axis=0, keepdims=True)
    lane = lax.broadcasted_iota(jnp.int32, (1, LANES), 1)
    term = [
        jnp.broadcast_to(jnp.sum(jnp.where(lane == i, total, 0.0), axis=1, keepdims=True), (ROWS, LANES))
        for i in range(7)
    ]
    held = term[1]
    moment = [term[0] + held] + [term[i] + held for i in range(2, 7)]
    c = coefficients(moment)
    both = c[0] + c[1] + c[2]
    for l in range(nl):
        slot = l % 2
        copies = [
            pltpu.make_async_copy(xs.at[slot], x.at[:, l], sem.at[slot, 0]),
            pltpu.make_async_copy(rs.at[slot], r.at[:, l], sem.at[slot, 1]),
        ]
        if l >= 2:
            for copy in copies:
                copy.wait()

        def chunk(u, _):
            for i in range(4):
                for h in range(2):
                    rows = pl.ds(pl.multiple_of(ROWS * (4 * u + i), ROWS), ROWS)
                    cols = pl.ds(LANES * h, LANES)
                    free = w[l, rows, cols] > 0.0
                    fx = jnp.where(free, c[0], both)
                    fr = jnp.where(free, 1.0, 1.0 - both)
                    for k in range(3):
                        b = raw[k, l, rows, cols]
                        v1, v2, v3 = m1[k, l, rows, cols], m2[k, l, rows, cols], m3[k, l, rows, cols]
                        xs[slot, k, rows, cols] = fx * b + (c[1] * v1 + c[2] * v2)
                        rs[slot, k, rows, cols] = fr * b - (c[0] * v1 + c[1] * v2 + c[2] * v3)
            return 0

        lax.fori_loop(0, nrow // (4 * ROWS), chunk, 0)
        for copy in copies:
            copy.start()
    for l in range(max(0, nl - 2), nl):
        slot = l % 2
        pltpu.make_async_copy(xs.at[slot], x.at[:, l], sem.at[slot, 0]).wait()
        pltpu.make_async_copy(rs.at[slot], r.at[:, l], sem.at[slot, 1]).wait()


def exchange(x, axis, first):
    peers = lax.axis_size(axis)
    pairs = []
    for i in range(first, peers - 1, 2):
        pairs += [(i, i + 1), (i + 1, i)]
    return lax.ppermute(x, axis, pairs)


def per_device(b, visc, strain, code):
    _, nl, nrow, nz = b.shape
    rows = nrow + ROWS
    par = jnp.stack([lax.axis_index("gx") % 2, lax.axis_index("yz") % 2]).astype(jnp.int32)
    peers = lax.axis_size("gx") * lax.axis_size("yz")
    S = jax.ShapeDtypeStruct

    ya, yb, xa, xb = call(
        pack_kernel, "pack",
        [("smem", par), ("hbm", b), ("hbm", visc), ("hbm", strain), ("hbm", code)],
        [resident((14, nl, ROWS, nz), BF16)] * 2 + [resident((13, nrow, nz), BF16)] * 2,
        scratch=[
            VMEM((2, 3, nl, ROWS, nz), F32), VMEM((2, nl, ROWS, nz), BF16), VMEM((2, 6, nl, ROWS, nz), BF16),
            VMEM((2, nl, ROWS, nz), jnp.int32), VMEM((2, 3, nrow, nz), F32), VMEM((2, nrow, nz), jnp.int32),
            pltpu.SemaphoreType.DMA((2, 8)),
        ],
        cost=(1e6, 2e6),
    )
    rya, ryb = exchange(ya, "yz", 0), exchange(yb, "yz", 1)
    rxa, rxb = exchange(xa, "gx", 0), exchange(xb, "gx", 1)

    raw, es, m0, w, acc0 = call(
        load_kernel, "load",
        [("hbm", b), ("hbm", visc), ("hbm", strain), ("hbm", code)],
        [
            resident((3, nl, nrow, nz)), resident((nl, 7, rows, nz)), resident((3, nl, rows, nz)),
            resident((nl, rows, nz)), resident((2, ROWS, LANES)),
        ],
        scratch=[
            VMEM((nl, nrow, nz), BF16), VMEM((nl, 6, nrow, nz), BF16), VMEM((nl, nrow, nz), jnp.int32),
            pltpu.SemaphoreType.DMA((nl, 4)),
        ],
        cost=(2e7, 9e6),
    )
    es, m0, w, ca, cb = call(
        halo_kernel, "halo",
        [("smem", par), ("v", rya), ("v", ryb), ("v", es), ("v", m0), ("v", w)],
        [
            resident((nl, 7, rows, nz)), resident((3, nl, rows, nz)), resident((nl, rows, nz)),
            resident((13, ROWS, nz), BF16), resident((13, ROWS, nz), BF16),
        ],
        aliases={3: 0, 4: 1, 5: 2},
    )
    rca, rcb = exchange(ca, "gx", 0), exchange(cb, "gx", 1)

    field = resident((3, nl, rows, nz))
    sums = resident((2, ROWS, LANES))
    plane = resident((3, rows, nz))
    tx_scratch = VMEM((3, rows, nz), F32)
    work = (4e7, 1e7)

    v, tx, acc = call(
        interior_kernel, "interior1", [("v", m0), ("v", es), ("v", w)], [field, plane, sums], cost=work
    )
    m1, acc1, low, ea, eb = call(
        first_boundary_kernel, "boundary1",
        [("smem", par), ("v", m0), ("v", es), ("v", w), ("v", rxa), ("v", rxb), ("v", rca), ("v", rcb),
         ("v", v), ("v", tx), ("v", acc)],
        [field, sums, resident((7, rows, nz)), plane, plane],
        scratch=[tx_scratch, tx_scratch, tx_scratch],
        aliases={8: 0},
    )
    ra, rb = exchange(ea, "gx", 0), exchange(eb, "gx", 1)
    v, tx, acc = call(
        interior_kernel, "interior2", [("v", m1), ("v", es), ("v", w)], [field, plane, sums], cost=work
    )
    m2, acc2, ea, eb = call(
        second_boundary_kernel, "boundary2",
        [("smem", par), ("v", m1), ("v", es), ("v", w), ("v", low), ("v", ra), ("v", rb),
         ("v", v), ("v", tx), ("v", acc)],
        [field, sums, plane, plane],
        scratch=[tx_scratch],
        aliases={7: 0},
    )
    ra, rb = exchange(ea, "gx", 0), exchange(eb, "gx", 1)
    v, tx, acc = call(
        interior_kernel, "interior3", [("v", m2), ("v", es), ("v", w)], [field, plane, sums], cost=work
    )
    m3, parts = call(
        third_boundary_kernel, "boundary3",
        [("smem", par), ("v", m2), ("v", es), ("v", w), ("v", low), ("v", ra), ("v", rb),
         ("v", v), ("v", tx), ("v", acc), ("v", acc0), ("v", acc1), ("v", acc2)],
        [field, resident((peers, LANES))],
        scratch=[tx_scratch, VMEM((2, ROWS, LANES), F32)],
        aliases={7: 0},
    )
    gathered = lax.all_to_all(parts, ("gx", "yz"), 0, 0)
    return call(
        output_kernel, "output",
        [("v", gathered), ("v", raw), ("v", w), ("v", m1), ("v", m2), ("v", m3)],
        [S(b.shape, F32), S(b.shape, F32)],
        scratch=[VMEM((2, 3, nrow, nz), F32), VMEM((2, 3, nrow, nz), F32), pltpu.SemaphoreType.DMA((2, 2))],
    )


def solution(mesh):
    placed = (
        P(None, "gx", "yz", None),
        P("gx", "yz", None),
        P(None, "gx", "yz", None),
        P("gx", "yz", None),
    )
    return jax.shard_map(
        per_device,
        mesh=mesh,
        in_specs=placed,
        out_specs=(P(None, "gx", "yz", None), P(None, "gx", "yz", None)),
        check_vma=False,
    )
```

```python
import functools

import jax
import jax.numpy as jnp
from jax import lax
from jax.experimental import pallas as pl
from jax.experimental.pallas import tpu as pltpu
from jax.sharding import PartitionSpec as P


SOFTEN = 0.8
F32 = jnp.float32
BF16 = jnp.bfloat16
LANES = 128
ROWS = 8
HALO = 3
VMEM = pltpu.VMEM


def resident(shape, dtype=F32):
    return VMEM(shape, dtype)


def in_vmem(x):
    return pltpu.with_memory_space_constraint(x, VMEM)


def call(kernel, ins, outs, scratch=(), aliases=None, limit=24, cost=(1e6, 1e6)):
    specs, args = [], []
    for kind, x in ins:
        if kind == "hbm":
            specs.append(pl.BlockSpec(memory_space=pltpu.HBM))
            args.append(pltpu.with_memory_space_constraint(x, pltpu.HBM))
        elif kind == "smem":
            specs.append(pl.BlockSpec(memory_space=pltpu.SMEM))
            args.append(x)
        else:
            specs.append(pl.BlockSpec(memory_space=VMEM))
            args.append(in_vmem(x))
    out_specs = [
        pl.BlockSpec(memory_space=VMEM) if isinstance(o, type(VMEM((8, 128), F32))) else pl.BlockSpec(memory_space=pltpu.HBM)
        for o in outs
    ]
    return pl.pallas_call(
        kernel,
        out_shape=outs,
        in_specs=specs,
        out_specs=out_specs,
        scratch_shapes=list(scratch),
        input_output_aliases=aliases or {},
        compiler_params=pltpu.CompilerParams(vmem_limit_bytes=limit << 20),
        cost_estimate=pl.CostEstimate(flops=int(cost[0]), bytes_accessed=int(cost[1]), transcendentals=0),
    )(*args)


def iotas():
    row = lax.broadcasted_iota(jnp.int32, (ROWS, LANES), 0)
    lane = lax.broadcasted_iota(jnp.int32, (ROWS, LANES), 1)
    return row, lane


def at(t, h):
    return pl.ds(ROWS * t, ROWS), pl.ds(LANES * h, LANES)


def weight_of(code):
    return jnp.where(code == 0, 0.0, jnp.where(code == 1, 0.2, 1.2)).astype(F32)


def tensor_of(visc, strain):
    two_eta = 2.0 * visc
    square = (
        strain[0] * strain[0]
        + strain[1] * strain[1]
        + strain[2] * strain[2]
        + 2.0 * (strain[3] * strain[3] + strain[4] * strain[4] + strain[5] * strain[5])
    )
    scale = jnp.sqrt(SOFTEN * two_eta / (1.0 + square))
    return [two_eta] + [scale * s for s in strain]


def split(x):
    high = x.astype(BF16)
    return high, (x - high.astype(F32)).astype(BF16)


def pack_y_kernel(par, b, visc, strain, code, ya, yb, token, tb, tv, ts, tc, sem):
    nl, nrow = b.shape[1], b.shape[2]
    py = par[1]
    copies = []
    for i, r in enumerate((0, nrow - ROWS)):
        rows = pl.ds(r, ROWS)
        copies.append(pltpu.make_async_copy(b.at[:, :, rows, :], tb.at[i], sem.at[i, 0]))
        copies.append(pltpu.make_async_copy(visc.at[:, rows, :], tv.at[i], sem.at[i, 1]))
        copies.append(pltpu.make_async_copy(strain.at[:, :, rows, :], ts.at[i], sem.at[i, 2]))
        copies.append(pltpu.make_async_copy(code.at[:, rows, :], tc.at[i], sem.at[i, 3]))
    for c in copies:
        c.start()
    token[...] = jnp.zeros(token.shape, F32)
    for c in copies:
        c.wait()
    row, _ = iotas()
    even = (py == 0).astype(jnp.int32) + jnp.zeros((ROWS, LANES), jnp.int32) == 1

    def layer(l, _):
        for h in range(2):
            cols = pl.ds(LANES * h, LANES)
            first, last = [], []
            for slot, planes in ((0, first), (1, last)):
                held = tc[slot, l, :, cols] == 0
                b3 = [split(jnp.where(held, 0.0, tb[slot, k, l, :, cols])) for k in range(3)]
                planes += [x[0].astype(F32) for x in b3] + [x[1].astype(F32) for x in b3]
                planes.append(tv[slot, l, :, cols].astype(F32))
                planes += [ts[slot, k, l, :, cols].astype(F32) for k in range(6)]
                planes.append(tc[slot, l, :, cols].astype(F32))
            last = [pltpu.roll(x, HALO, 0) for x in last]
            for out, up in ((ya, True), (yb, False)):
                planes = [jnp.where(even == up, y, x) for x, y in zip(first, last)]
                for j in range(3):
                    halves = []
                    for tile in (2 * j, 2 * j + 1):
                        value = jnp.zeros((ROWS, LANES), F32)
                        for k, x in enumerate(planes):
                            start = HALO * k - ROWS * tile
                            if start <= -HALO or start >= ROWS:
                                continue
                            moved = pltpu.roll(x, start % ROWS, 0) if start % ROWS else x
                            value = jnp.where((row >= start) & (row < start + HALO), moved, value)
                        halves.append(value)
                    out[l, pl.ds(16 * j, 16), cols] = jnp.concatenate(halves, 0).astype(BF16)
        return 0

    lax.fori_loop(0, nl, layer, 0)


def pack_x_kernel(par, b, visc, strain, code, token, xa, xb, lb, lc, sem):
    nl, nrow = b.shape[1], b.shape[2]
    px = par[0]
    copies = []
    late = []
    for i, out in enumerate((xa, xb)):
        layer = jnp.where(px == i, nl - 1, 0)
        copies.append(pltpu.make_async_copy(b.at[:, layer], lb.at[i], sem.at[i, 4]))
        copies.append(pltpu.make_async_copy(code.at[layer], lc.at[i], sem.at[i, 5]))
        late.append(pltpu.make_async_copy(visc.at[layer], out.at[6], sem.at[i, 6]))
        late.append(pltpu.make_async_copy(strain.at[:, layer], out.at[pl.ds(7, 6)], sem.at[i, 7]))
    for c in copies + late:
        c.start()
    for c in copies:
        c.wait()
    for i, out in enumerate((xa, xb)):
        for t in range(nrow // 16):
            rows = pl.ds(16 * t, 16)
            held = lc[i, rows, :] == 0
            for k in range(3):
                high, low = split(jnp.where(held, 0.0, lb[i, k, rows, :]))
                out[k, rows, :] = high
                out[3 + k, rows, :] = low
    for c in late:
        c.wait()


def load_kernel(b, visc, strain, code, raw, es, m0, w, acc, sv, ss, sc, sem):
    nl, nrow = b.shape[1], b.shape[2]

    def copies(l):
        return [
            pltpu.make_async_copy(b.at[:, l], raw.at[:, l], sem.at[l, 0]),
            pltpu.make_async_copy(visc.at[l], sv.at[l], sem.at[l, 1]),
            pltpu.make_async_copy(strain.at[:, l], ss.at[l], sem.at[l, 2]),
            pltpu.make_async_copy(code.at[l], sc.at[l], sem.at[l, 3]),
        ]

    for l in range(nl):
        for c in copies(l):
            c.start()
    zero = jnp.zeros((ROWS, LANES), F32)

    def layer(l, carry):
        whole, held = list(carry[0]), list(carry[1])
        for c in copies(l):
            c.wait()
        for u in range(nrow // 16):
            rows16 = pl.ds(16 * u, 16)
            v16 = sv[l, rows16, :].astype(F32)
            s16 = [ss[l, k, rows16, :].astype(F32) for k in range(6)]
            for i in range(2):
                for h in range(2):
                    cut = lambda x: x[ROWS * i : ROWS * (i + 1), LANES * h : LANES * (h + 1)]
                    rows, cols = pl.ds(16 * u + ROWS * i, ROWS), pl.ds(LANES * h, LANES)
                    weight = weight_of(sc[l, rows, cols])
                    w[l, rows, cols] = weight
                    for k, value in enumerate(tensor_of(cut(v16), [cut(s) for s in s16])):
                        es[l, k, rows, cols] = value
                    x = [raw[k, l, rows, cols] for k in range(3)]
                    for k in range(3):
                        m0[k, l, rows, cols] = jnp.where(weight > 0.0, x[k], 0.0)
                    square = x[0] * x[0] + x[1] * x[1] + x[2] * x[2]
                    j = 2 * i + h
                    whole[j] = whole[j] + square
                    held[j] = held[j] + jnp.where(weight > 0.0, 0.0, square)
        return tuple(whole), tuple(held)

    whole, held = lax.fori_loop(0, nl, layer, ((zero,) * 4, (zero,) * 4))
    acc[0] = (whole[0] + whole[1]) + (whole[2] + whole[3])
    acc[1] = (held[0] + held[1]) + (held[2] + held[3])


def halo_kernel(par, ra, rb, es_in, m0_in, w_in, es, m0, w, ca, cb):
    _, _ = iotas()
    row2 = lax.broadcasted_iota(jnp.int32, (ROWS, 2 * LANES), 0)
    nl = ra.shape[0]
    halo = es.shape[2] - ROWS
    px = par[0]
    py = par[1]
    rows = pl.ds(halo, ROWS)

    def planes(l):
        a, c = ra[l].astype(F32), rb[l].astype(F32)
        upper, lower = jnp.where(even3(a), a, c), jnp.where(even3(a), c, a)

        def moved(x, k, to):
            t, at_row = divmod(HALO * k, ROWS)
            part = x[ROWS * t : ROWS * (t + 1)]
            shift = (to - at_row) % ROWS
            part = pltpu.roll(part, shift, 0) if shift else part
            if at_row + HALO > ROWS:
                following = x[ROWS * (t + 1) : ROWS * (t + 2)]
                following = pltpu.roll(following, shift, 0) if shift else following
                part = jnp.where(row2 - to >= ROWS - at_row, following, part)
            return part

        return [
            jnp.where(row2 < HALO, moved(upper, k, 0), jnp.where(row2 >= ROWS - HALO, moved(lower, k, ROWS - HALO), 0.0))
            for k in range(14)
        ]

    def even3(x):
        return (py == 0).astype(jnp.int32) + jnp.zeros(x.shape, jnp.int32) == 1

    def layer(l, _):
        got = planes(l)
        w[l, rows, :] = weight_of(got[13])
        for k, value in enumerate(tensor_of(got[6], got[7:13])):
            es[l, k, rows, :] = value
        for k in range(3):
            m0[k, l, rows, :] = got[k] + got[3 + k]
        for i, out in enumerate((ca, cb)):

            @pl.when(l == jnp.where(px == i, nl - 1, 0))
            def _():
                for k in range(13):
                    out[k] = got[k].astype(BF16)

        return 0

    lax.fori_loop(0, nl, layer, 0)


def strain_parts(c, n, ynext, znext):
    ax = [n[k] - c[k] for k in range(3)]
    ay = [ynext[k] - c[k] for k in range(3)]
    az = [znext[k] - c[k] for k in range(3)]
    return [ax[0], ay[1], az[2], ay[0] + ax[1], az[0] + ax[2], az[1] + ay[2]]


def stress(parts, tensor, which):
    two_eta, s = tensor[0], tensor[1:]
    cross = (
        (s[0] * parts[0] + s[1] * parts[1])
        + (s[2] * parts[2] + s[3] * parts[3])
        + (s[4] * parts[4] + s[5] * parts[5])
    )
    eta = 0.5 * two_eta
    return {k: (two_eta if k < 3 else eta) * parts[k] - cross * s[k] for k in which}


class Plane:
    def __init__(self, center, following, tensor, tiles):
        self.center, self.following, self.tensor, self.tiles = center, following, tensor, tiles
        self.row, self.lane = iotas()
        self.cache = {}

    def rolled(self, t):
        if t not in self.cache:
            self.cache[t] = [[pltpu.roll(self.center(k, t, h), ROWS - 1, 0) for k in range(3)] for h in range(2)]
        return self.cache[t]

    def stresses(self, t, which):
        m = [[self.center(k, t, h) for k in range(3)] for h in range(2)]
        r, rn = self.rolled(t), self.rolled((t + 1) % self.tiles)
        del self.cache[t]
        z = [[pltpu.roll(m[h][k], LANES - 1, 1) for k in range(3)] for h in range(2)]
        out = []
        for h in range(2):
            ynext = [jnp.where(self.row == ROWS - 1, rn[h][k], r[h][k]) for k in range(3)]
            znext = [jnp.where(self.lane == LANES - 1, z[1][k] if h == 0 else 0.0, z[h][k]) for k in range(3)]
            n = [self.following(k, t, h) for k in range(3)]
            parts = strain_parts(m[h], n, ynext, znext)
            out.append(stress(parts, [self.tensor(k, t, h) for k in range(7)], which))
        return m, out


FLUX_X, FLUX_Y, FLUX_Z = (0, 3, 4), (3, 1, 5), (4, 5, 2)


def full_plane(plane, tx, weight, write, own):
    row, lane, tiles = plane.row, plane.lane, plane.tiles
    halo = tiles - 1
    before = None
    kept = None

    def flux(t):
        m, tau = plane.stresses(t, range(6))
        y = [[tau[h][j] for j in FLUX_Y] for h in range(2)]
        ry = [[pltpu.roll(v, 1, 0) for v in y[h]] for h in range(2)]
        rz = [[pltpu.roll(tau[h][j], 1, 1) for j in FLUX_Z] for h in range(2)]
        div = []
        for h in range(2):
            rows, cols = at(t, h)
            line = []
            for k in range(3):
                x = tau[h][FLUX_X[k]]
                prev_z = jnp.where(lane == 0, rz[0][k] if h == 1 else 0.0, rz[h][k])
                line.append((tx[k, rows, cols] - x) + (prev_z - tau[h][FLUX_Z[k]]) - y[h][k])
                tx[k, rows, cols] = x
            div.append(line)
        return m, ry, div

    def finish(t, m, ry, div, prev):
        for h in range(2):
            rows, cols = at(t, h)
            wt = weight(t, h)
            new = [
                jnp.where(
                    wt > 0.0,
                    div[h][k] + jnp.where(row == 0, prev[h][k], ry[h][k]) + wt * m[h][k],
                    0.0,
                )
                for k in range(3)
            ]
            for k in range(3):
                write(k, t, h, new[k])
            if t != halo and own is not None:
                own(t, h, m[h], new)

    kept = flux(halo)
    before = kept[1]
    for t in range(halo):
        m, ry, div = flux(t)
        finish(t, m, ry, div, before)
        before = ry
    finish(halo, kept[0], kept[1], kept[2], before)


def lower_flux(plane, emit):
    for t in range(plane.tiles):
        _, tau = plane.stresses(t, FLUX_X)
        for h in range(2):
            emit(t, h, [tau[h][j] for j in FLUX_X])


class Sums:
    def __init__(self, init, squares=True):
        self.cross = list(init[0])
        self.square = list(init[1])
        self.squares = squares

    def add(self, t, h, old, new):
        i = (2 * t + h) % len(self.cross)
        for k in range(3):
            self.cross[i] = self.cross[i] + old[k] * new[k]
            if self.squares:
                self.square[i] = self.square[i] + new[k] * new[k]

    def state(self):
        return (tuple(self.cross), tuple(self.square))


def interior_kernel(m, es, w, v, tx_out, acc, squares=True):
    nl, tiles = m.shape[1], m.shape[2] // ROWS
    zero = jnp.zeros((ROWS, LANES), F32)
    tx_out[...] = jnp.zeros(tx_out.shape, F32)

    def layer(l, carry):
        sums = Sums(carry, squares)
        plane = Plane(
            lambda k, t, h: m[(k, l) + at(t, h)],
            lambda k, t, h: m[(k, l + 1) + at(t, h)],
            lambda k, t, h: es[(l, k) + at(t, h)],
            tiles,
        )

        def write(k, t, h, value):
            v[(k, l) + at(t, h)] = value

        full_plane(plane, tx_out, lambda t, h: w[(l,) + at(t, h)], write, sums.add)
        keep = jnp.where(l > 0, 1.0, 0.0).astype(F32)
        return jax.tree.map(lambda s: s * keep, sums.state())

    start = ((zero, zero), (zero, zero))
    cross, square = lax.fori_loop(0, nl - 1, layer, start)
    acc[0] = cross[0] + cross[1]
    acc[1] = square[0] + square[1]


def boundary_body(m, es, w, lo, hi, low_tensor, v_in, tx_in, acc_in, v, tx, acc, squares=True):
    nl, tiles = m.shape[1], m.shape[2] // ROWS
    last = nl - 1
    zero = jnp.zeros((ROWS, LANES), F32)
    sums = Sums(((zero, zero), (zero, zero)), squares)

    below = Plane(lo, lambda k, t, h: m[(k, 0) + at(t, h)], low_tensor, tiles)

    def emit(t, h, flux):
        wt = w[(0,) + at(t, h)]
        new = []
        for k in range(3):
            value = v_in[(k, 0) + at(t, h)] + jnp.where(wt > 0.0, flux[k], 0.0)
            v[(k, 0) + at(t, h)] = value
            new.append(value)
        if t != tiles - 1:
            sums.add(t, h, [m[(k, 0) + at(t, h)] for k in range(3)], new)

    lower_flux(below, emit)
    for k in range(3):
        tx[k] = tx_in[k]
    top = Plane(
        lambda k, t, h: m[(k, last) + at(t, h)],
        hi,
        lambda k, t, h: es[(last, k) + at(t, h)],
        tiles,
    )

    def write(k, t, h, value):
        v[(k, last) + at(t, h)] = value

    full_plane(top, tx, lambda t, h: w[(last,) + at(t, h)], write, sums.add)
    acc[0] = acc_in[0] + sums.cross[0] + sums.cross[1]
    acc[1] = acc_in[1] + sums.square[0] + sums.square[1]


def choose(flag, a, b):
    return jnp.where(flag + jnp.zeros(a.shape, jnp.int32) == 1, a, b)


def send_planes(px, v, ea, eb):
    last = v.shape[1] - 1
    for i, out in enumerate((ea, eb)):
        l = jnp.where(px == i, last, 0)
        for k in range(3):
            out[k] = v[k, l]


def first_boundary_kernel(par, m, es, w, xa, xb, ca, cb, v_in, tx_in, acc_in, v, acc, low, ea, eb, lo_s, hi_s, tx):
    px = par[0]
    even = (px == 0).astype(jnp.int32)
    nrow = xa.shape[1]

    def unpack(a, b, rows):
        def side(k, up):
            x, y = a(k), b(k)
            return choose(even, x, y) if up else choose(even, y, x)

        for k in range(3):
            hi_s[k, rows, :] = side(k, True) + side(3 + k, True)
            lo_s[k, rows, :] = side(k, False) + side(3 + k, False)
        tensor = tensor_of(side(6, False), [side(7 + k, False) for k in range(6)])
        for k in range(7):
            low[k, rows, :] = tensor[k]

    for t in range(nrow // 16):
        rows = pl.ds(16 * t, 16)
        unpack(lambda k: xa[k, rows, :].astype(F32), lambda k: xb[k, rows, :].astype(F32), rows)
    unpack(lambda k: ca[k].astype(F32), lambda k: cb[k].astype(F32), pl.ds(nrow, ROWS))
    boundary_body(
        m, es, w,
        lambda k, t, h: lo_s[(k,) + at(t, h)],
        lambda k, t, h: hi_s[(k,) + at(t, h)],
        lambda k, t, h: low[(k,) + at(t, h)],
        v_in, tx_in, acc_in, v, tx, acc,
    )
    send_planes(px, v, ea, eb)


def later_boundary(par, m, es, w, low, ra, rb, v_in, tx_in, acc_in, v, acc, tx, squares=True):
    px = par[0]
    even = (px == 0).astype(jnp.int32)
    lo = lambda k, t, h: choose(even, rb[(k,) + at(t, h)], ra[(k,) + at(t, h)])
    hi = lambda k, t, h: choose(even, ra[(k,) + at(t, h)], rb[(k,) + at(t, h)])
    boundary_body(m, es, w, lo, hi, lambda k, t, h: low[(k,) + at(t, h)], v_in, tx_in, acc_in, v, tx, acc, squares)


def second_boundary_kernel(par, m, es, w, low, ra, rb, v_in, tx_in, acc_in, v, acc, ea, eb, tx):
    later_boundary(par, m, es, w, low, ra, rb, v_in, tx_in, acc_in, v, acc, tx)
    send_planes(par[0], v, ea, eb)


def third_boundary_kernel(
    par, m, es, w, low, ra, rb, v_in, tx_in, acc_in, acc0, acc1, acc2, v, parts, tx, acc
):
    later_boundary(par, m, es, w, low, ra, rb, v_in, tx_in, acc_in, v, acc, tx, False)
    _, lane = iotas()
    line = jnp.zeros((ROWS, LANES), F32)
    terms = [acc0[0], acc0[1], acc1[0], acc1[1], acc2[0], acc2[1], acc[0]]
    for i, value in enumerate(terms):
        total = jnp.sum(jnp.sum(value, axis=0, keepdims=True), axis=1, keepdims=True)
        line = jnp.where(lane == i, total, line)
    for t in range(parts.shape[0] // ROWS):
        parts[pl.ds(ROWS * t, ROWS), :] = line


def coefficients(moment):
    size = 4
    zero = None

    def dot(a, b, shift):
        total = None
        for i in range(size):
            for j in range(size):
                if a[i] is None or b[j] is None:
                    continue
                term = a[i] * b[j] * moment[i + j + shift]
                total = term if total is None else total + term
        return total

    def axpy(a, scale, b):
        out = []
        for x, y in zip(a, b):
            term = None if y is None else scale * y
            out.append(x if term is None else term if x is None else x + term)
        return out

    one = jnp.ones_like(moment[0])
    residual = [one, zero, zero, zero]
    direction = list(residual)
    field = [zero] * size
    now = moment[0]
    for iteration in range(3):
        alpha = now / dot(direction, direction, 1)
        field = axpy(field, alpha, direction)
        if iteration == 2:
            break
        residual = axpy(residual, -alpha, [None] + direction[: size - 1])
        following = dot(residual, residual, 0)
        direction = axpy(residual, following / now, direction)
        now = following
    return field[:3]


def output_kernel(gathered, raw, w, m1, m2, m3, x, r, xs, rs, sem):
    nl, nrow = raw.shape[1], raw.shape[2]
    total = jnp.sum(gathered[...], axis=0, keepdims=True)
    lane = lax.broadcasted_iota(jnp.int32, (1, LANES), 1)
    term = [
        jnp.broadcast_to(jnp.sum(jnp.where(lane == i, total, 0.0), axis=1, keepdims=True), (ROWS, LANES))
        for i in range(7)
    ]
    held = term[1]
    moment = [term[0]] + [term[i] + held for i in range(2, 7)]
    c = coefficients(moment)
    both = c[0] + c[1] + c[2]
    rest = 1.0 - both

    def copies(l):
        return [
            pltpu.make_async_copy(xs.at[l], x.at[:, l], sem.at[l, 0]),
            pltpu.make_async_copy(rs.at[l], r.at[:, l], sem.at[l, 1]),
        ]

    def layer(l, _):
        for t in range(nrow // ROWS):
            for h in range(2):
                rows, cols = at(t, h)
                free = w[l, rows, cols] > 0.0
                fx = jnp.where(free, c[0], both)
                fr = jnp.where(free, 1.0, rest)
                for k in range(3):
                    b = raw[k, l, rows, cols]
                    v1, v2, v3 = m1[k, l, rows, cols], m2[k, l, rows, cols], m3[k, l, rows, cols]
                    xs[l, k, rows, cols] = fx * b + (c[1] * v1 + c[2] * v2)
                    rs[l, k, rows, cols] = fr * b - (c[0] * v1 + c[1] * v2 + c[2] * v3)
        for copy in copies(l):
            copy.start()
        return 0

    lax.fori_loop(0, nl, layer, 0)
    for l in range(nl):
        for copy in copies(l):
            copy.wait()


def exchange(x, axis, first):
    peers = lax.axis_size(axis)
    pairs = []
    for i in range(first, peers - 1, 2):
        pairs += [(i, i + 1), (i + 1, i)]
    return lax.ppermute(x, axis, pairs)


def device_program(b, visc, strain, code):
    _, nl, nrow, nz = b.shape
    rows = nrow + ROWS
    par = jnp.stack([lax.axis_index("gx") % 2, lax.axis_index("yz") % 2]).astype(jnp.int32)
    peers = lax.axis_size("gx") * lax.axis_size("yz")
    S = jax.ShapeDtypeStruct

    inputs = [("hbm", b), ("hbm", visc), ("hbm", strain), ("hbm", code)]
    ya, yb, token = call(
        pack_y_kernel, [("smem", par)] + inputs,
        [resident((nl, 48, nz), BF16)] * 2 + [resident((ROWS, LANES))],
        scratch=[
            VMEM((2, 3, nl, ROWS, nz), F32), VMEM((2, nl, ROWS, nz), BF16), VMEM((2, 6, nl, ROWS, nz), BF16),
            VMEM((2, nl, ROWS, nz), jnp.int32), pltpu.SemaphoreType.DMA((2, 4)),
        ],
        cost=(1e6, 2e6),
    )
    rya, ryb = exchange(ya, "yz", 0), exchange(yb, "yz", 1)
    xa, xb = call(
        pack_x_kernel, [("smem", par)] + inputs + [("v", token)],
        [resident((13, nrow, nz), BF16)] * 2,
        scratch=[VMEM((2, 3, nrow, nz), F32), VMEM((2, nrow, nz), jnp.int32), pltpu.SemaphoreType.DMA((2, 8))],
        cost=(1e6, 2e6),
    )
    rxa, rxb = exchange(xa, "gx", 0), exchange(xb, "gx", 1)

    raw, es, m0, w, acc0 = call(
        load_kernel, inputs,
        [
            resident((3, nl, nrow, nz)), resident((nl, 7, rows, nz)), resident((3, nl, rows, nz)),
            resident((nl, rows, nz)), resident((2, ROWS, LANES)),
        ],
        scratch=[
            VMEM((nl, nrow, nz), BF16), VMEM((nl, 6, nrow, nz), BF16), VMEM((nl, nrow, nz), jnp.int32),
            pltpu.SemaphoreType.DMA((nl, 4)),
        ],
        cost=(2e7, 9e6),
    )
    es, m0, w, ca, cb = call(
        halo_kernel,
        [("smem", par), ("v", rya), ("v", ryb), ("v", es), ("v", m0), ("v", w)],
        [
            resident((nl, 7, rows, nz)), resident((3, nl, rows, nz)), resident((nl, rows, nz)),
            resident((13, ROWS, nz), BF16), resident((13, ROWS, nz), BF16),
        ],
        aliases={3: 0, 4: 1, 5: 2},
    )
    rca, rcb = exchange(ca, "gx", 0), exchange(cb, "gx", 1)

    field = resident((3, nl, rows, nz))
    sums = resident((2, ROWS, LANES))
    plane = resident((3, rows, nz))
    tx_scratch = VMEM((3, rows, nz), F32)
    work = (4e7, 1e7)

    v, tx, acc = call(interior_kernel, [("v", m0), ("v", es), ("v", w)], [field, plane, sums], cost=work)
    m1, acc1, low, ea, eb = call(
        first_boundary_kernel,
        [("smem", par), ("v", m0), ("v", es), ("v", w), ("v", rxa), ("v", rxb), ("v", rca), ("v", rcb),
         ("v", v), ("v", tx), ("v", acc)],
        [field, sums, resident((7, rows, nz)), plane, plane],
        scratch=[tx_scratch, tx_scratch, tx_scratch],
        aliases={8: 0},
    )
    ra, rb = exchange(ea, "gx", 0), exchange(eb, "gx", 1)
    v, tx, acc = call(interior_kernel, [("v", m1), ("v", es), ("v", w)], [field, plane, sums], cost=work)
    m2, acc2, ea, eb = call(
        second_boundary_kernel,
        [("smem", par), ("v", m1), ("v", es), ("v", w), ("v", low), ("v", ra), ("v", rb),
         ("v", v), ("v", tx), ("v", acc)],
        [field, sums, plane, plane],
        scratch=[tx_scratch],
        aliases={7: 0},
    )
    ra, rb = exchange(ea, "gx", 0), exchange(eb, "gx", 1)
    v, tx, acc = call(
        functools.partial(interior_kernel, squares=False), [("v", m2), ("v", es), ("v", w)], [field, plane, sums], cost=work
    )
    m3, parts = call(
        third_boundary_kernel,
        [("smem", par), ("v", m2), ("v", es), ("v", w), ("v", low), ("v", ra), ("v", rb),
         ("v", v), ("v", tx), ("v", acc), ("v", acc0), ("v", acc1), ("v", acc2)],
        [field, resident((peers, LANES))],
        scratch=[tx_scratch, VMEM((2, ROWS, LANES), F32)],
        aliases={7: 0},
    )
    gathered = lax.all_to_all(parts, ("gx", "yz"), 0, 0)
    return call(
        output_kernel,
        [("v", gathered), ("v", raw), ("v", w), ("v", m1), ("v", m2), ("v", m3)],
        [S(b.shape, F32), S(b.shape, F32)],
        scratch=[VMEM((nl, 3, nrow, nz), F32), VMEM((nl, 3, nrow, nz), F32), pltpu.SemaphoreType.DMA((nl, 2))],
    )


def solution(mesh):
    placed = (
        P(None, "gx", "yz", None),
        P("gx", "yz", None),
        P(None, "gx", "yz", None),
        P("gx", "yz", None),
    )
    return jax.shard_map(
        device_program,
        mesh=mesh,
        in_specs=placed,
        out_specs=(P(None, "gx", "yz", None), P(None, "gx", "yz", None)),
        check_vma=False,
    )
```
